32 devices in a mesh: row: 2 (over y), col: 4 (over z), depth: 4 (over x, core).
Axes of the slice: x: 2, y: 2, z: 4, core: 2. Of those that a mesh axis runs over, the one named last changes fastest.
Arguments:
- tokens: bfloat16 [512, 12288], P(('row', 'col'), 'depth'), may hold values from -6 to 6
- weight: bfloat16 [12288, 24576], P('depth', ('row', 'col')), may hold values from -5 to 5
- moment: bfloat16 [12288, 24576], P('depth', ('row', 'col')), may hold values from -0.59765625 to 0.59765625
- upstream: bfloat16 [2, 256, 24576], P(None, 'col', ('row', 'depth')), may hold values from -24 to 24
Outputs:
- activated: bfloat16 [2, 256, 24576], P(None, 'col', ('row', 'depth'))
- new_weight: bfloat16 [12288, 24576], P('depth', ('row', 'col'))
- new_moment: bfloat16 [12288, 24576], P('depth', ('row', 'col'))
The draws below stay inside these ranges and needn't reach their ends.
All inputs are finite; a program needn't handle non-finite values.
Results may differ from the reference program's by a relative error of at most 0.015.
Values may be sent and summed in bfloat16 or wider, within the bound.
No kernel may reach another device: no remote copies, remote signals or barrier semaphores. Data moves between devices by JAX's collectives and lax.ppermute only.
A program may use at most 256 MiB of HBM per device.

```python
import jax
import jax.numpy as jnp
from jax import lax

D = 12288
FF = 24576
TOK_DEV = 64
TOKENS = 512
N_ROW = 2
N_COL = 4
N_DEPTH = 4


def block_scale(rng, shape, pieces, smallest, high):
    def one(axis_at, parts):
        steps = jax.random.uniform(jax.random.fold_in(jax.random.fold_in(rng, 6), axis_at), (parts,), jnp.float32, smallest / len(pieces), high / len(pieces))
        return jnp.repeat(jnp.exp(steps), shape[axis_at] // parts).reshape((-1,) + (1,) * (len(shape) - axis_at - 1))

    loudness = one(*pieces[0])
    for cut in pieces[1:]:
        loudness = loudness * one(*cut)
    return loudness


def bell_draw(key, extent, scale, reach, cuts=(), kind=jnp.bfloat16):
    entries = scale * jax.random.normal(key, extent, jnp.float32)
    if cuts:
        entries = entries * block_scale(key, extent, cuts, -0.22, 0.18)
    return jnp.clip(entries, -reach, reach).astype(kind)


def setup_inputs(seed: int = 0) -> dict:
    keys = jax.random.split(jax.random.key(seed), 5)
    return {
        "tokens": bell_draw(keys[0], (TOKENS, D), 1.0, 6.0, ((0, 8), (1, 4))),
        "weight": bell_draw(keys[1], (D, FF), 1.0, 5.0, ((0, 4), (1, 8))),
        "moment": bell_draw(keys[2], (D, FF), 0.1, 0.59765625, ((0, 4), (1, 8))),
        "upstream": bell_draw(keys[3], (N_ROW, N_COL * TOK_DEV, FF), 4.0, 24.0, ((1, 4), (2, 8))),
    }


gelu_coef = 0.7978845608028654
cubic_coef = 0.044715
lion_rate = 0.5
decay_rate = 0.1
beta_one = 0.9
beta_two = 0.99
smooth_tau = 0.1

def gelu_pair(preact):
    tangent = jnp.tanh(gelu_coef * (preact + cubic_coef * preact * preact * preact))
    gelu_value = 0.5 * preact * (1.0 + tangent)
    gelu_slope = 0.5 * (1.0 + tangent) + 0.5 * preact * (1.0 - tangent * tangent) * gelu_coef * (1.0 + 3.0 * cubic_coef * preact * preact)
    return (gelu_value, gelu_slope)

def reference(tokens, weight, moment, upstream):
    block_width = D // N_DEPTH
    tokens_f = tokens.astype(jnp.float32)
    weight_f = weight.astype(jnp.float32)
    summed = jnp.zeros((TOKENS, FF), jnp.float32)
    for block in range(N_DEPTH):
        part = jnp.dot(tokens_f[:, block * block_width:(block + 1) * block_width], weight_f[block * block_width:(block + 1) * block_width, :], precision=lax.Precision.HIGHEST)
        summed = summed + lax.optimization_barrier(part.astype(jnp.bfloat16)).astype(jnp.float32)
    fan_scale = D ** (-0.5)
    gelu_value, gelu_slope = gelu_pair(summed * fan_scale)
    activated = gelu_value.astype(jnp.bfloat16).reshape(N_ROW, N_COL * TOK_DEV, FF)
    upstream_flat = upstream.reshape(TOKENS, FF).astype(jnp.float32)
    act_grad = (upstream_flat * gelu_slope).astype(jnp.bfloat16)
    grad_full = lax.dot_general(tokens_f, act_grad.astype(jnp.float32), (((0,), (0,)), ((), ())), precision=lax.Precision.HIGHEST) * fan_scale
    moment_f = moment.astype(jnp.float32)
    blended = beta_one * moment_f + (1.0 - beta_one) * grad_full
    update = blended / jnp.sqrt(blended * blended + smooth_tau * smooth_tau)
    new_weight = (weight_f - lion_rate * (update + decay_rate * weight_f)).astype(jnp.bfloat16)
    new_moment = (beta_two * moment_f + (1.0 - beta_two) * grad_full).astype(jnp.bfloat16)
    return (activated, new_weight, new_moment)
```

```python
import functools

import jax
import jax.numpy as jnp
from jax import lax
from jax.experimental import pallas as pl
from jax.experimental.pallas import tpu as pltpu
from jax.sharding import PartitionSpec as P

gelu_coef = 0.7978845608028654
cubic_coef = 0.044715
lion_rate = 0.5
decay_rate = 0.1
beta_one = 0.9
beta_two = 0.99
smooth_tau = 0.1


def gelu_pair(preact):
    tangent = jnp.tanh(gelu_coef * (preact + cubic_coef * preact * preact * preact))
    gelu_value = 0.5 * preact * (1.0 + tangent)
    gelu_slope = 0.5 * (1.0 + tangent) + 0.5 * preact * (1.0 - tangent * tangent) * gelu_coef * (
        1.0 + 3.0 * cubic_coef * preact * preact
    )
    return (gelu_value, gelu_slope)


def tile_of(extent, unit, most):
    best = extent
    for size in range(unit, min(extent, most) + 1, unit):
        if extent % size == 0:
            best = size
    return best


def lion_kernel(strip, fan_scale, flipped, grads, weight, moment, new_weight, new_moment):
    columns = weight.shape[1]
    for start in range(0, columns, strip):
        here = slice(start, start + strip)
        grad = jnp.dot(flipped[...], grads[:, here], preferred_element_type=jnp.float32) * fan_scale
        moment_f = moment[:, here].astype(jnp.float32)
        weight_f = weight[:, here].astype(jnp.float32)
        blended = beta_one * moment_f + (1.0 - beta_one) * grad
        update = blended * lax.rsqrt(blended * blended + smooth_tau * smooth_tau)
        kept = (1.0 - lion_rate * decay_rate) * weight_f
        new_weight[:, here] = (kept - lion_rate * update).astype(new_weight.dtype)
        new_moment[:, here] = (beta_two * moment_f + (1.0 - beta_two) * grad).astype(new_moment.dtype)


def lion_step(flipped, grads, weight, moment, fan_scale):
    rows, columns = weight.shape
    count = flipped.shape[1]
    tall = tile_of(rows, 128, 256)
    strip = tile_of(columns, 128, 512)
    block = pl.BlockSpec((tall, columns), lambda i: (i, 0))
    return pl.pallas_call(
        functools.partial(lion_kernel, strip, fan_scale),
        grid=(rows // tall,),
        in_specs=[
            pl.BlockSpec((tall, count), lambda i: (i, 0)),
            pl.BlockSpec((count, columns), lambda i: (0, 0)),
            block,
            block,
        ],
        out_specs=[block, block],
        out_shape=[
            jax.ShapeDtypeStruct(weight.shape, weight.dtype),
            jax.ShapeDtypeStruct(moment.shape, moment.dtype),
        ],
        compiler_params=pltpu.CompilerParams(vmem_limit_bytes=40 * 1024 * 1024),
        cost_estimate=pl.CostEstimate(
            flops=2 * rows * columns * count,
            bytes_accessed=8 * rows * columns,
            transcendentals=rows * columns,
        ),
        name="lion_step",
    )(flipped, grads, weight, moment)


def shards(tokens, weight, moment, upstream):
    row_count = lax.axis_size("row")
    col_count = lax.axis_size("col")
    depth_count = lax.axis_size("depth")
    pieces = depth_count // col_count
    tok_rows, width = tokens.shape
    held = row_count * tok_rows
    columns = upstream.shape[2]
    fan_scale = (width * depth_count) ** (-0.5)
    swap = [
        (c * depth_count + d, (d // pieces) * depth_count + c * pieces + d % pieces)
        for c in range(col_count)
        for d in range(depth_count)
    ]
    upstream_here = lax.ppermute(upstream.reshape(held, columns), ("col", "depth"), swap)
    every_token = lax.all_gather(tokens, ("row", "col"), axis=0, tiled=True)
    ordered = (
        every_token.reshape(row_count, col_count, tok_rows, width)
        .transpose(1, 0, 2, 3)
        .reshape(col_count * held, width)
    )
    partial_value = jnp.dot(ordered, weight, preferred_element_type=jnp.float32).astype(jnp.bfloat16)
    if pieces > 1:
        partial_value = (
            partial_value.reshape(col_count, held, pieces, columns)
            .transpose(0, 2, 1, 3)
            .reshape(depth_count * held, columns)
        )
    summed = lax.psum_scatter(partial_value, "depth", scatter_dimension=0, tiled=True).astype(jnp.float32)
    gelu_value, gelu_slope = gelu_pair(summed * fan_scale)
    activated = lax.ppermute(gelu_value.astype(jnp.bfloat16), ("col", "depth"), swap)
    local_grad = (upstream_here.astype(jnp.float32) * gelu_slope).astype(jnp.bfloat16)
    act_grad = lax.all_gather(local_grad, "depth", axis=0, tiled=True)
    if pieces > 1:
        act_grad = (
            act_grad.reshape(col_count, pieces, held, columns)
            .transpose(0, 2, 1, 3)
            .reshape(col_count * held, pieces * columns)
        )
    new_weight, new_moment = lion_step(ordered.T, act_grad, weight, moment, fan_scale)
    return (activated.reshape(upstream.shape), new_weight, new_moment)


def solution(mesh):
    assert mesh.shape["depth"] % mesh.shape["col"] == 0
    placed = (
        P(("row", "col"), "depth"),
        P("depth", ("row", "col")),
        P("depth", ("row", "col")),
        P(None, "col", ("row", "depth")),
    )
    return jax.shard_map(
        shards,
        mesh=mesh,
        in_specs=placed,
        out_specs=(
            P(None, "col", ("row", "depth")),
            P("depth", ("row", "col")),
            P("depth", ("row", "col")),
        ),
        check_vma=False,
    )
```

```python
import functools

import jax
import jax.numpy as jnp
from jax import lax
from jax.experimental import pallas as pl
from jax.experimental.pallas import tpu as pltpu
from jax.sharding import PartitionSpec as P


gelu_coef = 0.7978845608028654
cubic_coef = 0.044715
lion_rate = 0.5
decay_rate = 0.1
beta_one = 0.9
beta_two = 0.99
smooth_tau = 0.1


def gelu_pair(preact):
    tangent = jnp.tanh(gelu_coef * (preact + cubic_coef * preact * preact * preact))
    gelu_value = 0.5 * preact * (1.0 + tangent)
    gelu_slope = 0.5 * (1.0 + tangent) + 0.5 * preact * (1.0 - tangent * tangent) * gelu_coef * (
        1.0 + 3.0 * cubic_coef * preact * preact
    )
    return (gelu_value, gelu_slope)


def tile_of(extent, unit, most):
    best = extent
    for size in range(unit, min(extent, most) + 1, unit):
        if extent % size == 0:
            best = size
    return best


def reverse_bits(value, bits):
    return sum(((value >> b) & 1) << (bits - 1 - b) for b in range(bits))


def fetch_kernel(parts, source, target, sems):
    tall = source.shape[0] // parts
    copies = [
        pltpu.make_async_copy(
            source.at[pl.ds(i * tall, tall)], target.at[pl.ds(i * tall, tall)], sems.at[i]
        )
        for i in range(parts)
    ]
    for copy in copies:
        copy.start()
    for copy in copies:
        copy.wait()


def fetch(value):
    parts = 4
    return pl.pallas_call(
        functools.partial(fetch_kernel, parts),
        in_specs=[pl.BlockSpec(memory_space=pltpu.HBM)],
        out_specs=pl.BlockSpec(memory_space=pltpu.VMEM),
        out_shape=pltpu.VMEM(value.shape, value.dtype),
        scratch_shapes=[pltpu.SemaphoreType.DMA((parts,))],
        compiler_params=pltpu.CompilerParams(vmem_limit_bytes=1024 * 1024),
        cost_estimate=pl.CostEstimate(flops=0, bytes_accessed=value.size * 2, transcendentals=0),
    )(pltpu.with_memory_space_constraint(value, pltpu.HBM))


def order_kernel(wanted, *refs):
    col_count = lax.axis_size("col")
    blocks, (ordered, flipped) = refs[:-2], refs[-2:]
    tall = blocks[0].shape[0]
    for j, which in enumerate(wanted()):
        away = lax.rem(which - lax.axis_index("col") + col_count, col_count)
        for o, block in enumerate(blocks):

            @pl.when(away == o)
            def _(j=j, block=block):
                ordered[j * tall : (j + 1) * tall, :] = block[...]

    width = ordered.shape[1]
    wide = tile_of(width, 128, 256)
    for start in range(0, width, wide):
        flipped[start : start + wide, :] = ordered[:, start : start + wide].T


def order_tokens(wanted, blocks):
    tall, width = blocks[0].shape
    count = tall * len(blocks)
    kind = blocks[0].dtype
    whole = pl.BlockSpec(memory_space=pltpu.VMEM)
    return pl.pallas_call(
        functools.partial(order_kernel, wanted),
        in_specs=[whole] * len(blocks),
        out_specs=[whole, whole],
        out_shape=[pltpu.VMEM((count, width), kind), pltpu.VMEM((width, count), kind)],
        compiler_params=pltpu.CompilerParams(vmem_limit_bytes=12 * 1024 * 1024),
        cost_estimate=pl.CostEstimate(flops=0, bytes_accessed=6 * count * width, transcendentals=0),
        name="order_tokens",
    )(*blocks)


def lion_kernel(shape, strip, fan_scale, *refs):
    chunks, pieces = shape
    flipped, held = refs[:chunks], refs[chunks : chunks * (1 + pieces)]
    weight, moment, new_weight, new_moment, grads = refs[chunks * (1 + pieces) :]
    tall = held[0].shape[0]

    @pl.when(pl.program_id(0) == 0)
    def _():
        for i, piece in enumerate(held):
            grads[i * tall : (i + 1) * tall, :] = piece[...]

    count = tall * pieces
    kind = new_weight.dtype
    for start in range(0, new_weight.shape[1], strip):
        here = slice(start, start + strip)
        grad = sum(
            jnp.dot(f[...], grads[j * count : (j + 1) * count, here], preferred_element_type=jnp.float32)
            for j, f in enumerate(flipped)
        )
        old, kept = moment[:, here], weight[:, here]
        change = (grad * fan_scale).astype(kind) - old
        blended = old + jnp.asarray(1.0 - beta_one, kind) * change
        update = blended * lax.rsqrt(blended * blended + jnp.asarray(smooth_tau * smooth_tau, kind))
        new_weight[:, here] = kept - jnp.asarray(lion_rate, kind) * (update + jnp.asarray(decay_rate, kind) * kept)
        new_moment[:, here] = old + jnp.asarray(1.0 - beta_two, kind) * change


def lion_step(flipped, held, weight, moment, fan_scale):
    rows, columns = weight.shape
    tall = tile_of(rows, 128, 256)
    strip = tile_of(columns, 128, 512)
    block = pl.BlockSpec((tall, columns), lambda i: (i, 0))
    parts = [piece for chunk in held for piece in chunk]
    count = sum(f.shape[1] for f in flipped)
    return pl.pallas_call(
        functools.partial(lion_kernel, (len(held), len(held[0])), strip, fan_scale),
        grid=(rows // tall,),
        in_specs=[pl.BlockSpec((tall, f.shape[1]), lambda i: (i, 0)) for f in flipped]
        + [pl.BlockSpec(p.shape, lambda i: (0, 0), pipeline_mode=pl.Buffered(1)) for p in parts]
        + [block, block],
        out_specs=[block, block],
        out_shape=[
            jax.ShapeDtypeStruct(weight.shape, weight.dtype),
            jax.ShapeDtypeStruct(moment.shape, moment.dtype),
        ],
        scratch_shapes=[pltpu.VMEM((count, columns), weight.dtype)],
        compiler_params=pltpu.CompilerParams(vmem_limit_bytes=40 * 1024 * 1024),
        cost_estimate=pl.CostEstimate(
            flops=2 * rows * columns * count,
            bytes_accessed=8 * rows * columns,
            transcendentals=rows * columns,
        ),
        name="lion_step",
    )(*flipped, *parts, weight, moment)


def shards(tokens, weight, moment, upstream):
    row_count = lax.axis_size("row")
    col_count = lax.axis_size("col")
    depth_count = lax.axis_size("depth")
    row, depth = lax.axis_index("row"), lax.axis_index("depth")
    pieces = depth_count // col_count
    bits = depth_count.bit_length() - 1
    tok_rows, width = tokens.shape
    columns = upstream.shape[2]
    fan_scale = (width * depth_count) ** (-0.5)

    near = fetch(weight)

    if pieces == 1:
        set_of, part_of = [reverse_bits(q, bits) for q in range(depth_count)], [0] * depth_count
    else:
        set_of = [q // pieces for q in range(depth_count)]
        part_of = [q % pieces for q in range(depth_count)]
    piece_at = {(set_of[q], part_of[q]): q for q in range(depth_count)}
    home = [
        (c * depth_count + q, set_of[q] * depth_count + c * pieces + part_of[q])
        for c in range(col_count)
        for q in range(depth_count)
    ]
    away = [(b, a) for a, b in home]
    order = [reverse_bits(j, bits) for j in range(depth_count)]

    def wanted():
        if pieces > 1:
            return [jnp.int32(t) for t in range(col_count)]
        here = lax.axis_index("depth")
        return [
            sum(((here ^ q) >> b & 1) << (bits - 1 - b) for b in range(bits)) for q in order
        ]

    def flip(value, bit):
        return lax.ppermute(value, "depth", [(q, q ^ (1 << bit)) for q in range(depth_count)])

    up = [(c, (c + 1) % col_count) for c in range(col_count)]
    down = [(b, a) for a, b in up]
    ring = [(r, (r - 1) % row_count) for r in range(row_count)]

    first = {0: tokens}
    from_above = from_below = tokens
    for step in range(1, (col_count + 1) // 2):
        from_above = lax.ppermute(from_above, "col", down)
        from_below = lax.ppermute(from_below, "col", up)
        first[step], first[col_count - step] = from_above, from_below
    if col_count > 1 and col_count % 2 == 0:
        half = tok_rows // 2
        first[col_count // 2] = jnp.concatenate(
            [lax.ppermute(from_above[:half], "col", down), lax.ppermute(from_below[half:], "col", up)]
        )
    upstream, _ = lax.optimization_barrier((upstream, first[col_count // 2]))
    blocks = [[first[o] for o in range(col_count)]]
    for _ in range(1, row_count):
        blocks.append([lax.ppermute(b, "row", ring) for b in blocks[-1]])

    flipped, grads, values = [], [], []
    for j in range(row_count):
        ordered, turned = order_tokens(wanted, blocks[j])
        if pieces == 1:
            count = ordered.shape[0] // 2
            sent = jnp.dot(ordered[count:], near, preferred_element_type=jnp.float32).astype(jnp.bfloat16)
            kept = jnp.dot(ordered[:count], near, preferred_element_type=jnp.float32)
        else:
            partial_value = jnp.dot(ordered, near, preferred_element_type=jnp.float32)
            partial_value = partial_value.reshape(col_count, tok_rows, pieces, columns).transpose(0, 2, 1, 3)
            partial_value = jnp.concatenate(
                [
                    lax.dynamic_index_in_dim(
                        partial_value.reshape(depth_count, tok_rows, columns), depth ^ q, 0, keepdims=False
                    )
                    for q in order
                ]
            )
            count = partial_value.shape[0] // 2
            sent, kept = partial_value[count:].astype(jnp.bfloat16), partial_value[:count]
        for bit in range(bits):
            kept = kept + flip(sent, bit).astype(jnp.float32)
            if bit + 1 < bits:
                count = kept.shape[0] // 2
                sent, kept = kept[count:].astype(jnp.bfloat16), kept[:count]
        gelu_value, gelu_slope = gelu_pair(kept * fan_scale)
        values.append(lax.ppermute(gelu_value.astype(jnp.bfloat16), ("col", "depth"), home))
        theirs = lax.dynamic_index_in_dim(upstream, lax.rem(row + j, row_count), 0, keepdims=False)
        theirs = lax.ppermute(theirs, ("col", "depth"), away).astype(jnp.float32)
        held = [(theirs * gelu_slope).astype(jnp.bfloat16)]
        for bit in reversed(range(bits)):
            held = held + [flip(h, bit) for h in held]
        if pieces > 1:
            stacked = jnp.stack(held)
            table = jnp.array([order.index(q) for q in range(depth_count)], jnp.int32)
            grad = jnp.stack(
                [
                    lax.dynamic_index_in_dim(stacked, table[depth ^ piece_at[t, p]], 0, keepdims=False)
                    for t in range(col_count)
                    for p in range(pieces)
                ]
            )
            grad = grad.reshape(col_count, pieces, tok_rows, columns).transpose(0, 2, 1, 3)
            held = [grad.reshape(col_count * tok_rows, pieces * columns)]
        flipped.append(turned)
        grads.append(held)
    new_weight, new_moment = lion_step(flipped, grads, weight, moment, fan_scale)
    twice = jnp.stack(values + values)
    activated = lax.dynamic_slice_in_dim(twice, row_count - row, row_count, axis=0)
    return (activated, new_weight, new_moment)


def solution(mesh):
    depth_count, col_count = mesh.shape["depth"], mesh.shape["col"]
    assert depth_count % col_count == 0 and depth_count & (depth_count - 1) == 0
    placed = (
        P(("row", "col"), "depth"),
        P("depth", ("row", "col")),
        P("depth", ("row", "col")),
        P(None, "col", ("row", "depth")),
    )

    return jax.shard_map(
        shards,
        mesh=mesh,
        in_specs=placed,
        out_specs=(
            P(None, "col", ("row", "depth")),
            P("depth", ("row", "col")),
            P("depth", ("row", "col")),
        ),
        check_vma=False,
    )
```

```python
import functools

import jax
import jax.numpy as jnp
from jax import lax
from jax.experimental import pallas as pl
from jax.experimental.pallas import tpu as pltpu
from jax.sharding import PartitionSpec as P


near = pl.BlockSpec(memory_space=pltpu.VMEM)

gelu_coef = 0.7978845608028654
cubic_coef = 0.044715
lion_rate = 0.5
decay_rate = 0.1
beta_one = 0.9
beta_two = 0.99
smooth_tau = 0.1


def gelu_pair(preact):
    tangent = jnp.tanh(gelu_coef * (preact + cubic_coef * preact * preact * preact))
    gelu_value = 0.5 * preact * (1.0 + tangent)
    gelu_slope = 0.5 * (1.0 + tangent) + 0.5 * preact * (1.0 - tangent * tangent) * gelu_coef * (
        1.0 + 3.0 * cubic_coef * preact * preact
    )
    return (gelu_value, gelu_slope)


def tile_of(extent, unit, most):
    best = extent
    for size in range(unit, min(extent, most) + 1, unit):
        if extent % size == 0:
            best = size
    return best


def reverse_bits(value, bits):
    return sum(((value >> b) & 1) << (bits - 1 - b) for b in range(bits))


def far(value):
    return pltpu.with_memory_space_constraint(value, pltpu.HBM)


def mix_kernel(wanted, *refs):
    col_count = lax.axis_size("col")
    *blocks, weight, flipped, kept, sent, ordered, stored, sems = refs
    tall = blocks[0].shape[0]
    _, width = ordered.shape
    parts, _, strip = stored.shape
    copies = [
        pltpu.make_async_copy(weight.at[:, pl.ds(i * strip, strip)], stored.at[i], sems.at[i])
        for i in range(parts)
    ]
    for copy in copies:
        copy.start()
    for j, which in enumerate(wanted()):
        away = lax.rem(which - lax.axis_index("col") + col_count, col_count)
        for o, block in enumerate(blocks):

            @pl.when(away == o)
            def _(j=j, block=block):
                ordered[j * tall : (j + 1) * tall, :] = block[...]

    wide = tile_of(width, 128, 256)
    for start in range(0, width, wide):
        flipped[start : start + wide, :] = ordered[:, start : start + wide].T

    rows = kept.shape[0]
    for i in range(parts):
        copies[i].wait()
        here = slice(i * strip, (i + 1) * strip)
        value = jnp.dot(ordered[...], stored[i], preferred_element_type=jnp.float32)
        kept[:, here] = value[:rows]
        sent[:, here] = value[rows:].astype(sent.dtype)


def mix(wanted, blocks, weight):
    tall, width = blocks[0].shape
    count = tall * len(blocks)
    columns = weight.shape[1]
    kind = weight.dtype
    strip = tile_of(columns, 128, 512)
    parts = columns // strip
    return pl.pallas_call(
        functools.partial(mix_kernel, wanted),
        in_specs=[near] * len(blocks) + [pl.BlockSpec(memory_space=pltpu.HBM)],
        out_specs=[near] * 3,
        out_shape=[
            jax.ShapeDtypeStruct((width, count), kind),
            jax.ShapeDtypeStruct((count // 2, columns), jnp.float32),
            jax.ShapeDtypeStruct((count // 2, columns), kind),
        ],
        scratch_shapes=[
            pltpu.VMEM((count, width), kind),
            pltpu.VMEM((parts, width, strip), kind),
            pltpu.SemaphoreType.DMA((parts,)),
        ],
        compiler_params=pltpu.CompilerParams(vmem_limit_bytes=32 * 1024 * 1024),
        cost_estimate=pl.CostEstimate(
            flops=2 * count * width * columns, bytes_accessed=2 * width * columns, transcendentals=0
        ),
        name="mix",
    )(*blocks, far(weight))


def fold_kernel(strip, old, arrived, kept, sent):
    half = kept.shape[0]
    for start in range(0, old.shape[1], strip):
        here = slice(start, start + strip)
        value = old[:, here] + arrived[:, here].astype(jnp.float32)
        kept[:, here] = value[:half]
        sent[:, here] = value[half:].astype(sent.dtype)


def fold(old, arrived):
    rows, columns = arrived.shape
    return pl.pallas_call(
        functools.partial(fold_kernel, tile_of(columns, 128, 256)),
        out_shape=[
            jax.ShapeDtypeStruct((rows // 2, columns), jnp.float32),
            jax.ShapeDtypeStruct((rows // 2, columns), arrived.dtype),
        ],
        compiler_params=pltpu.CompilerParams(vmem_limit_bytes=8 * 1024 * 1024),
        cost_estimate=pl.CostEstimate(flops=rows * columns, bytes_accessed=8 * rows * columns, transcendentals=0),
        name="fold",
    )(old, arrived)


def slope_kernel(strip, fan_scale, kept, arrived, upstream, value, grad):
    for start in range(0, kept.shape[1], strip):
        here = slice(start, start + strip)
        preact = (kept[:, here] + arrived[:, here].astype(jnp.float32)) * fan_scale
        gelu_value, gelu_slope = gelu_pair(preact)
        value[:, here] = gelu_value.astype(value.dtype)
        grad[:, here] = (upstream[:, here].astype(jnp.float32) * gelu_slope * fan_scale).astype(grad.dtype)


def slope(kept, arrived, upstream, fan_scale):
    shape, kind = arrived.shape, arrived.dtype
    return pl.pallas_call(
        functools.partial(slope_kernel, tile_of(shape[1], 128, 256), fan_scale),
        out_shape=[jax.ShapeDtypeStruct(shape, kind)] * 2,
        compiler_params=pltpu.CompilerParams(vmem_limit_bytes=8 * 1024 * 1024),
        cost_estimate=pl.CostEstimate(
            flops=30 * shape[0] * shape[1], bytes_accessed=0, transcendentals=shape[0] * shape[1]
        ),
        name="slope",
    )(kept, arrived, upstream)


def lion_kernel(shape, strip, *refs):
    chunks, pieces = shape
    flipped, held = refs[:chunks], refs[chunks : chunks * (1 + pieces)]
    weight, moment, new_weight, new_moment, left, grads, weights, moments, sems = refs[chunks * (1 + pieces) :]
    tall = left.shape[0]
    steps = weights.shape[0] // tall
    kind = weights.dtype

    def copies(step, back):
        rows = pl.ds(pl.multiple_of(step * tall, tall), tall)
        pairs = ((weights, new_weight), (moments, new_moment)) if back else ((weight, weights), (moment, moments))
        return [
            pltpu.make_async_copy(a.at[rows], b.at[rows], sems.at[2 * back + k, step])
            for k, (a, b) in enumerate(pairs)
        ]

    @pl.loop(0, steps)
    def _(step):
        for copy in copies(step, 0):
            copy.start()

    high = held[0].shape[0]
    for i, piece in enumerate(held):
        grads[i * high : (i + 1) * high, :] = piece[...]
    count = high * pieces

    @pl.loop(0, steps)
    def _(step):
        for copy in copies(step, 0):
            copy.wait()
        rows = pl.ds(pl.multiple_of(step * tall, tall), tall)
        for j, f in enumerate(flipped):
            left[:, j * count : (j + 1) * count] = f[rows, :]
        for start in range(0, weights.shape[1], strip):
            here = slice(start, start + strip)
            grad = jnp.dot(left[...], grads[:, here], preferred_element_type=jnp.float32).astype(kind)
            old, kept = moments[rows, here], weights[rows, here]
            change = grad - old
            blended = old + jnp.asarray(1.0 - beta_one, kind) * change
            update = blended * lax.rsqrt(blended * blended + jnp.asarray(smooth_tau * smooth_tau, kind))
            weights[rows, here] = kept - jnp.asarray(lion_rate, kind) * (
                update + jnp.asarray(decay_rate, kind) * kept
            )
            moments[rows, here] = old + jnp.asarray(1.0 - beta_two, kind) * change
        for copy in copies(step, 1):
            copy.start()

    @pl.loop(0, steps)
    def _(step):
        for copy in copies(step, 1):
            copy.wait()


def lion_step(flipped, held, weight, moment):
    rows, columns = weight.shape
    tall = tile_of(rows, 128, 256)
    strip = tile_of(columns, 128, 256)
    parts = [piece for chunk in held for piece in chunk]
    count = sum(f.shape[1] for f in flipped)
    there = pl.BlockSpec(memory_space=pltpu.HBM)
    kind = weight.dtype
    return pl.pallas_call(
        functools.partial(lion_kernel, (len(held), len(held[0])), strip),
        in_specs=[near] * (len(flipped) + len(parts)) + [there] * 2,
        out_specs=[there] * 2,
        out_shape=[
            jax.ShapeDtypeStruct(weight.shape, weight.dtype),
            jax.ShapeDtypeStruct(moment.shape, moment.dtype),
        ],
        scratch_shapes=[
            pltpu.VMEM((tall, count), kind),
            pltpu.VMEM((count, columns), kind),
            pltpu.VMEM((rows, columns), kind),
            pltpu.VMEM((rows, columns), kind),
            pltpu.SemaphoreType.DMA((4, rows // tall)),
        ],
        compiler_params=pltpu.CompilerParams(vmem_limit_bytes=54 * 1024 * 1024),
        cost_estimate=pl.CostEstimate(
            flops=2 * rows * columns * count,
            bytes_accessed=8 * rows * columns,
            transcendentals=rows * columns,
        ),
        name="lion_step",
    )(*flipped, *parts, far(weight), far(moment))


def shards(tokens, weight, moment, upstream):
    row_count = lax.axis_size("row")
    col_count = lax.axis_size("col")
    depth_count = lax.axis_size("depth")
    row, depth = lax.axis_index("row"), lax.axis_index("depth")
    pieces = depth_count // col_count
    bits = depth_count.bit_length() - 1
    tok_rows, width = tokens.shape
    columns = upstream.shape[2]
    fan_scale = (width * depth_count) ** (-0.5)

    if pieces == 1:
        set_of, part_of = [reverse_bits(q, bits) for q in range(depth_count)], [0] * depth_count
    else:
        set_of = [q // pieces for q in range(depth_count)]
        part_of = [q % pieces for q in range(depth_count)]
    piece_at = {(set_of[q], part_of[q]): q for q in range(depth_count)}
    home = [
        (c * depth_count + q, set_of[q] * depth_count + c * pieces + part_of[q])
        for c in range(col_count)
        for q in range(depth_count)
    ]
    away = [(b, a) for a, b in home]
    order = [reverse_bits(j, bits) for j in range(depth_count)]

    def wanted():
        if pieces > 1:
            return [jnp.int32(t) for t in range(col_count)]
        here = lax.axis_index("depth")
        return [
            sum(((here ^ q) >> b & 1) << (bits - 1 - b) for b in range(bits)) for q in order
        ]

    def flip(value, bit):
        return lax.ppermute(value, "depth", [(q, q ^ (1 << bit)) for q in range(depth_count)])

    up = [(c, (c + 1) % col_count) for c in range(col_count)]
    down = [(b, a) for a, b in up]
    ring = [(r, (r - 1) % row_count) for r in range(row_count)]

    first = {0: tokens}
    from_above = from_below = tokens
    for step in range(1, (col_count + 1) // 2):
        from_above = lax.ppermute(from_above, "col", down)
        from_below = lax.ppermute(from_below, "col", up)
        first[step], first[col_count - step] = from_above, from_below
    if col_count > 1 and col_count % 2 == 0:
        half = tok_rows // 2
        above_half = lax.ppermute(from_above[:half], "col", down)
        below_half = lax.ppermute(from_below[half:], "col", up)
        first[col_count // 2] = jnp.concatenate([above_half, below_half])
    blocks = [[first[o] for o in range(col_count)]]
    for _ in range(1, row_count):
        passed = []
        for block in blocks[-1]:
            passed.append(lax.ppermute(block, "row", ring))
        blocks.append(passed)

    flipped, grads, values = [], [], []
    for j in range(row_count):
        turned, kept, sent = mix(wanted, blocks[j], weight)
        if pieces > 1:
            partial_value = jnp.concatenate([kept, sent.astype(jnp.float32)])
            partial_value = partial_value.reshape(col_count, tok_rows, pieces, columns).transpose(0, 2, 1, 3)
            partial_value = partial_value.reshape(depth_count, tok_rows, columns)
            partial_value = jnp.concatenate(
                [lax.dynamic_index_in_dim(partial_value, depth ^ q, 0, keepdims=False) for q in order]
            )
            count = partial_value.shape[0] // 2
            kept, sent = partial_value[:count], partial_value[count:].astype(jnp.bfloat16)
        for bit in range(bits - 1):
            arrived = flip(sent, bit)
            kept, sent = fold(kept, arrived)
        theirs = lax.dynamic_index_in_dim(upstream, lax.rem(row + j, row_count), 0, keepdims=False)
        theirs = lax.ppermute(theirs, ("col", "depth"), away)
        gelu_value, grad = slope(kept, flip(sent, bits - 1), theirs, fan_scale)
        held = [grad]
        values.append(lax.ppermute(gelu_value, ("col", "depth"), home))
        for bit in reversed(range(bits)):
            held = held + [flip(h, bit) for h in held]
        if pieces > 1:
            stacked = jnp.stack(held)
            table = jnp.array([order.index(q) for q in range(depth_count)], jnp.int32)
            grad = jnp.stack(
                [
                    lax.dynamic_index_in_dim(stacked, table[depth ^ piece_at[t, p]], 0, keepdims=False)
                    for t in range(col_count)
                    for p in range(pieces)
                ]
            )
            grad = grad.reshape(col_count, pieces, tok_rows, columns).transpose(0, 2, 1, 3)
            held = [grad.reshape(col_count * tok_rows, pieces * columns)]
        flipped.append(turned)
        grads.append(held)
    new_weight, new_moment = lion_step(flipped, grads, weight, moment)
    twice = jnp.stack(values + values)
    activated = lax.dynamic_slice_in_dim(twice, row_count - row, row_count, axis=0)
    return (activated, new_weight, new_moment)


def solution(mesh):
    depth_count, col_count = mesh.shape["depth"], mesh.shape["col"]
    assert depth_count % col_count == 0 and depth_count & (depth_count - 1) == 0
    placed = (
        P(("row", "col"), "depth"),
        P("depth", ("row", "col")),
        P("depth", ("row", "col")),
        P(None, "col", ("row", "depth")),
    )

    return jax.shard_map(
        shards,
        mesh=mesh,
        in_specs=placed,
        out_specs=(
            P(None, "col", ("row", "depth")),
            P("depth", ("row", "col")),
            P("depth", ("row", "col")),
        ),
        check_vma=False,
    )
```
